256 devices in a mesh: tm: 32 (over z, x), height: 8 (over y, core).
Axes of the slice: x: 4, y: 4, z: 8, core: 2. Of those that a mesh axis runs over, the one named last changes fastest.
Arguments:
- latents: bfloat16 [64, 64, 104, 256], P('tm', 'height'), may hold values from -45 to 45
- first_gain: bfloat16 [256], replicated, may hold values from 0.099609375 to 1.8984375
- first_kernel: bfloat16 [3, 3, 3, 256, 256], replicated, may hold values from -0.078125 to 0.078125
- first_bias: bfloat16 [256], replicated, may hold values from -3 to 3
- second_gain: bfloat16 [256], replicated, may hold values from 0.099609375 to 1.8984375
- second_kernel: bfloat16 [3, 3, 3, 256, 256], replicated, may hold values from -0.078125 to 0.078125
- second_bias: bfloat16 [256], replicated, may hold values from -3 to 3
Outputs:
- decoded: bfloat16 [64, 64, 104, 256], P('tm', 'height')
The draws below stay inside these ranges and needn't reach their ends.
All inputs are finite; a program needn't handle non-finite values.
Results may differ from the reference program's by a relative error of at most 0.0055.
Values may be sent and summed in bfloat16 or wider, within the bound.
A program may use at most 64 MiB of HBM per device.

```python
import math
import jax
import jax.numpy as jnp
from jax import lax

CH = 256
W = 104
FRAMES = 64
ROWS = 64


def draw_latents(key, part):
    key_base, key_spot, key_chan = jax.random.split(key, 3)
    frame_pos = jnp.arange(FRAMES, dtype=jnp.float32) / max(FRAMES - 1, 1)
    row_pos = jnp.arange(ROWS, dtype=jnp.float32) / max(ROWS - 1, 1)
    ramp = (1.0 + frame_pos)[:, None, None, None] * (1.0 + 0.8 * row_pos)[None, :, None, None]
    base = jnp.clip(jax.random.normal(key_base, (FRAMES, ROWS, W, CH), jnp.float32), -3.5, 3.5)
    spot = jnp.exp(jax.random.uniform(key_spot, (FRAMES, ROWS, W, 1), jnp.float32, 0.0, math.log(3.2)))
    chan = jnp.exp(jax.random.uniform(key_chan, (CH,), jnp.float32, -math.log(3.2), math.log(3.2)))
    return (0.25 * base * ramp * spot * chan).astype(jnp.bfloat16)


def noise(rng, shape, deviation, limit, kind=jnp.bfloat16):
    return jnp.clip(deviation * jax.random.normal(rng, shape, jnp.float32), -limit, limit).astype(kind)


def setup_inputs(seed: int = 0) -> dict:
    keys = jax.random.split(jax.random.key(seed), 8)
    return {
        "latents": draw_latents(jax.random.fold_in(keys[7], 71), 0),
        "first_gain": jnp.clip(1.0 + 0.18 * jax.random.normal(keys[1], (CH,), jnp.float32), 0.099609375, 1.8984375).astype(jnp.bfloat16),
        "first_kernel": noise(keys[2], (3, 3, 3, CH, CH), (27 * CH) ** -0.5, 0.078125),
        "first_bias": noise(keys[3], (CH,), 0.5, 3.0),
        "second_gain": jnp.clip(1.0 + 0.18 * jax.random.normal(keys[4], (CH,), jnp.float32), 0.099609375, 1.8984375).astype(jnp.bfloat16),
        "second_kernel": noise(keys[5], (3, 3, 3, CH, CH), (27 * CH) ** -0.5, 0.078125),
        "second_bias": noise(keys[6], (CH,), 0.5, 3.0),
    }


EPSILON = 1e-06

def normalize(field, gain):
    mean_power = lax.optimization_barrier(jnp.mean(jnp.square(field), axis=-1, keepdims=True))
    return field * lax.rsqrt(mean_power + EPSILON) * gain.astype(jnp.float32)

def activate(field, gain):
    return jax.nn.silu(normalize(field, gain)).astype(jnp.bfloat16)

def causal_conv(acts, kernel, bias):
    padded = jnp.pad(acts, ((2, 0), (1, 1), (1, 1), (0, 0)))
    bias_f = bias.astype(jnp.float32)

    def one_frame(frame_idx):
        total = jnp.zeros((ROWS * W, CH), jnp.float32)
        for tap_time in range(3):
            slab = lax.dynamic_slice_in_dim(padded, frame_idx + tap_time, 1, 0)[0]
            for tap_row in range(3):
                columns = jnp.concatenate([slab[tap_row:tap_row + ROWS, tap_col:tap_col + W] for tap_col in range(3)], -1)
                columns = columns.reshape(ROWS * W, 3 * CH)
                taps = kernel[tap_time, tap_row].reshape(3 * CH, CH)
                total = total + jnp.dot(columns, taps, preferred_element_type=jnp.float32)
        return total.reshape(ROWS, W, CH) + bias_f
    return lax.map(one_frame, jnp.arange(FRAMES, dtype=jnp.int32))

def reference(latents, first_gain, first_kernel, first_bias, second_gain, second_kernel, second_bias):
    field = latents.astype(jnp.float32)
    first_act = activate(field, first_gain)
    first_out = causal_conv(first_act, first_kernel, first_bias).astype(jnp.bfloat16)
    middle = first_out.astype(jnp.float32)
    second_act = activate(middle, second_gain)
    second_out = causal_conv(second_act, second_kernel, second_bias)
    return (field + second_out).astype(jnp.bfloat16)
```

```python
import functools

import jax
import jax.numpy as jnp
from jax import lax
from jax.experimental import pallas as pl
from jax.experimental.pallas import tpu as pltpu
from jax.sharding import PartitionSpec as P

EPSILON = 1e-06
MESH = pl.DeviceIdType.MESH
F32 = jnp.float32


def kernel(
    tm_size, height_size,
    lat, gain1, gain2, bias1, bias2, w1_hbm, w2_hbm,
    out,
    latv, w1, w2, halo, ledge, sendbuf, lhs, acc, outv,
    load_sem, out_sem, tm_send, tm_recv, hl_send, hl_recv, hf_send, hf_recv,
):
    frames, rows, cells, channels = latv.shape
    wide = lhs.shape[3]
    tm = lax.axis_index("tm")
    ht = lax.axis_index("height")
    has_prev = tm > 0
    has_next = tm < tm_size - 1
    has_up = ht > 0
    has_down = ht < height_size - 1

    load_lat = pltpu.make_async_copy(lat, latv, load_sem.at[0])
    load_w1 = pltpu.make_async_copy(w1_hbm, w1, load_sem.at[1])
    load_w2 = pltpu.make_async_copy(w2_hbm, w2, load_sem.at[2])
    load_lat.start()
    load_w1.start()
    load_w2.start()

    nxt = jnp.minimum(tm + 1, tm_size - 1)
    prv = jnp.maximum(tm - 1, 0)
    up = jnp.maximum(ht - 1, 0)
    down = jnp.minimum(ht + 1, height_size - 1)

    barrier = pltpu.get_barrier_semaphore()
    for exists, there in (
        (has_prev, {"tm": prv}), (has_next, {"tm": nxt}),
        (has_up, {"height": up}), (has_down, {"height": down}),
    ):
        @pl.when(exists)
        def _(there=there):
            pl.semaphore_signal(barrier, inc=1, device_id=there, device_id_type=MESH)
    peers = sum(h.astype(jnp.int32) for h in (has_prev, has_next, has_up, has_down))
    pl.semaphore_wait(barrier, peers)

    def source(e, row):
        return lat.at[:, row] if e == 0 else sendbuf.at[row]

    def tm_copy(e, row):
        return pltpu.make_async_remote_copy(
            src_ref=source(e, row), dst_ref=halo.at[e, row + 1],
            send_sem=tm_send.at[e, row], recv_sem=tm_recv.at[e, row],
            device_id={"tm": nxt}, device_id_type=MESH)

    def local_edge(e, side):
        return pltpu.make_async_remote_copy(
            src_ref=source(e, 0 if side == 0 else rows - 1), dst_ref=ledge.at[e, side],
            send_sem=hl_send.at[e, side], recv_sem=hl_recv.at[e, side],
            device_id={"height": up if side == 0 else down}, device_id_type=MESH)

    def halo_edge(e, side):
        return pltpu.make_async_remote_copy(
            src_ref=halo.at[e, 1 if side == 0 else rows],
            dst_ref=halo.at[e, rows + 1 if side == 0 else 0],
            send_sem=hf_send.at[e, side], recv_sem=hf_recv.at[e, side],
            device_id={"height": up if side == 0 else down}, device_id_type=MESH)

    to_side = (has_up, has_down)
    from_side = (has_down, has_up)

    def start_tm(e, row):
        @pl.when(has_next)
        def _():
            tm_copy(e, row).start()

    def start_local_edge(e, side):
        @pl.when(to_side[side])
        def _():
            local_edge(e, side).start()

    start_local_edge(0, 0)
    start_local_edge(0, 1)

    def send_row(i, carry):
        start_tm(0, lax.rem(i + rows - 1, rows))
        return carry

    lax.fori_loop(0, rows, send_row, 0)

    g1 = gain1[...].astype(F32)
    g2 = gain2[...].astype(F32)
    b1 = bias1[...].astype(F32)
    b2 = bias2[...].astype(F32)

    def activate(values, gain):
        power = jnp.mean(jnp.square(values), axis=-1, keepdims=True)
        return jax.nn.silu(values * lax.rsqrt(power + EPSILON) * gain)

    pad = jnp.zeros((wide - cells, channels), F32)

    def expand(e, frame, row, values):
        v = jnp.concatenate([values, pad], 0)
        lhs[e, frame, row, :, :channels] = pltpu.roll(v, 1, 0).astype(jnp.bfloat16)
        lhs[e, frame, row, :, channels:2 * channels] = v.astype(jnp.bfloat16)
        lhs[e, frame, row, :, 2 * channels:] = pltpu.roll(v, wide - 1, 0).astype(jnp.bfloat16)

    def clear(e, frame, row):
        lhs[e, frame, row] = jnp.zeros((wide, 3 * channels), jnp.bfloat16)

    def take(e, frame, row, raw):
        values = raw.astype(F32)
        if e == 0:
            values = activate(values, g1)
        expand(e, frame, row, values)

    def take_halo(e, row):
        @pl.when(has_prev)
        def _():
            tm_copy(e, row).wait_recv()
        for side, edge in ((0, 0), (1, rows - 1)):
            if isinstance(row, int) and row == edge:
                @pl.when(has_prev & to_side[side])
                def _(side=side):
                    halo_edge(e, side).start()

        @pl.when(has_prev)
        def _():
            for f in range(2):
                take(e, f, row + 1, halo[e, row + 1, f])

        @pl.when(jnp.logical_not(has_prev))
        def _():
            for f in range(2):
                clear(e, f, row + 1)

    def take_halo_edge(e, side):
        row = rows + 1 if side == 0 else 0
        there = has_prev & from_side[side]

        @pl.when(there)
        def _():
            halo_edge(e, side).wait_recv()
            for f in range(2):
                take(e, f, row, halo[e, row, f])

        @pl.when(jnp.logical_not(there))
        def _():
            for f in range(2):
                clear(e, f, row)

    def take_local_edge(e, side):
        row = rows + 1 if side == 0 else 0

        @pl.when(from_side[side])
        def _():
            local_edge(e, side).wait_recv()
            for f in range(2):
                take(e, 2 + f, row, ledge[e, side, f])

        @pl.when(jnp.logical_not(from_side[side]))
        def _():
            for f in range(2):
                clear(e, 2 + f, row)

    def tap(e, w, frame, row, count, i, j):
        block = lhs[e, frame, pl.ds(row + j, count)].reshape(count * wide, 3 * channels)
        return jnp.dot(block, w[i * 3 + j], preferred_element_type=F32)

    def local_conv(e, w, count):
        def chunk(c, carry):
            row = c * count
            first = sum(tap(e, w, 2, row, count, 2, j) for j in range(3))
            acc[e, 0, pl.ds(row, count)] = first.reshape(count, wide, channels)
            second = sum(
                tap(e, w, 2, row, count, 1, j) + tap(e, w, 3, row, count, 2, j) for j in range(3))
            acc[e, 1, pl.ds(row, count)] = second.reshape(count, wide, channels)
            return carry
        lax.fori_loop(0, rows // count, chunk, 0)

    def halo_conv(e, w, row):
        first = acc[e, 0, row] + sum(
            tap(e, w, 0, row, 1, 0, j) + tap(e, w, 1, row, 1, 1, j) for j in range(3))
        second = acc[e, 1, row] + sum(tap(e, w, 1, row, 1, 0, j) for j in range(3))
        return first[:cells], second[:cells]

    load_lat.wait()

    def own_row(row, carry):
        for f in range(2):
            take(0, 2 + f, row + 1, latv[f, row])
        return carry

    lax.fori_loop(0, rows, own_row, 0)
    take_local_edge(0, 0)
    take_local_edge(0, 1)
    load_w1.wait()
    local_conv(0, w1, 4)

    def middle_row(row):
        for f, v in enumerate(halo_conv(0, w1, row)):
            a = activate((v + b1).astype(jnp.bfloat16).astype(F32), g2)
            sendbuf[row, f] = a.astype(jnp.bfloat16)
            expand(1, 2 + f, row + 1, a)

    take_halo(0, rows - 1)
    take_halo(0, 0)
    take_halo_edge(0, 0)
    take_halo_edge(0, 1)

    def middle_step(r, carry):
        take_halo(0, r)
        middle_row(r - 1)

        @pl.when(r > 1)
        def _():
            start_tm(1, r - 2)
        return carry

    lax.fori_loop(1, rows - 2, middle_step, 0)
    start_local_edge(1, 0)
    take_halo(0, rows - 2)
    start_tm(1, rows - 4)
    middle_row(rows - 1)
    middle_row(rows - 3)
    start_tm(1, rows - 1)
    start_local_edge(1, 1)
    middle_row(rows - 2)
    start_tm(1, rows - 3)
    take_local_edge(1, 0)
    start_tm(1, rows - 2)
    take_local_edge(1, 1)
    load_w2.wait()
    local_conv(1, w2, 4)

    def out_copy(row):
        return pltpu.make_async_copy(outv.at[:, row], out.at[:, row], out_sem.at[row])

    def last_row(row):
        for f, v in enumerate(halo_conv(1, w2, row)):
            outv[f, row] = (latv[f, row].astype(F32) + (v + b2)).astype(jnp.bfloat16)
        out_copy(row).start()

    take_halo(1, 0)

    def last_step(r, carry):
        take_halo(1, r)

        @pl.when(r > 1)
        def _():
            last_row(r - 1)
        return carry

    lax.fori_loop(1, rows - 3, last_step, 0)
    take_halo(1, rows - 1)
    take_halo(1, rows - 3)
    last_row(rows - 4)
    take_halo_edge(1, 1)
    last_row(0)
    take_halo_edge(1, 0)
    take_halo(1, rows - 2)
    last_row(rows - 3)
    last_row(rows - 2)
    last_row(rows - 1)

    def drain(row, carry):
        out_copy(row).wait()

        @pl.when(has_next)
        def _():
            tm_copy(0, row).wait_send()
            tm_copy(1, row).wait_send()
        return carry

    lax.fori_loop(0, rows, drain, 0)
    for e in range(2):
        for side in range(2):
            @pl.when(to_side[side])
            def _(e=e, side=side):
                local_edge(e, side).wait_send()

            @pl.when(has_prev & to_side[side])
            def _(e=e, side=side):
                halo_edge(e, side).wait_send()


def per_device(
    tm_size, height_size,
    latents, first_gain, first_kernel, first_bias, second_gain, second_kernel, second_bias,
):
    frames, rows, cells, channels = latents.shape
    wide = -(-(cells + 1) // 16) * 16
    vmem = pl.BlockSpec(memory_space=pltpu.VMEM)
    hbm = pl.BlockSpec(memory_space=pl.ANY)
    bf16 = jnp.bfloat16
    dma = pltpu.SemaphoreType.DMA
    row = lambda v: v.reshape(1, channels)
    taps = lambda k: k.reshape(9, 3 * channels, channels)
    return pl.pallas_call(
        functools.partial(kernel, tm_size, height_size),
        out_shape=jax.ShapeDtypeStruct(latents.shape, bf16),
        in_specs=[hbm, vmem, vmem, vmem, vmem, hbm, hbm],
        out_specs=hbm,
        scratch_shapes=[
            pltpu.VMEM(latents.shape, bf16),
            pltpu.VMEM((9, 3 * channels, channels), bf16),
            pltpu.VMEM((9, 3 * channels, channels), bf16),
            pltpu.VMEM((2, rows + 2, 2, cells, channels), bf16),
            pltpu.VMEM((2, 2, 2, cells, channels), bf16),
            pltpu.VMEM((rows, 2, cells, channels), bf16),
            pltpu.VMEM((2, 4, rows + 2, wide, 3 * channels), bf16),
            pltpu.VMEM((2, 2, rows, wide, channels), F32),
            pltpu.VMEM(latents.shape, bf16),
            dma((3,)), dma((rows,)),
            dma((2, rows)), dma((2, rows)),
            dma((2, 2)), dma((2, 2)), dma((2, 2)), dma((2, 2)),
        ],
        compiler_params=pltpu.CompilerParams(
            collective_id=0, has_side_effects=True, vmem_limit_bytes=60 * 1024 * 1024),
        name="residual_block",
    )(latents, row(first_gain), row(second_gain), row(first_bias), row(second_bias),
      taps(first_kernel), taps(second_kernel))


def solution(mesh):
    return jax.shard_map(
        functools.partial(per_device, mesh.shape["tm"], mesh.shape["height"]),
        mesh=mesh,
        in_specs=(P("tm", "height", None, None), P(), P(), P(), P(), P(), P()),
        out_specs=P("tm", "height", None, None),
        check_vma=False,
    )
```

```python
import functools

import jax
import jax.numpy as jnp
from jax import lax
from jax.experimental import pallas as pl
from jax.experimental.pallas import tpu as pltpu
from jax.sharding import PartitionSpec as P

EPSILON = 1e-06
MESH = pl.DeviceIdType.MESH
F32 = jnp.float32


def kernel(
    tm_size, height_size,
    lat, gain1, gain2, bias1, bias2, w1_hbm, w2_hbm,
    out,
    latv, w1, w2, halo, ledge, sendbuf, lhs, acc,
    load_sem, tm_send, tm_recv, hl_send, hl_recv, hf_send, hf_recv,
):
    frames, rows, cells, channels = latv.shape
    wide = lhs.shape[3]
    tm = lax.axis_index("tm")
    ht = lax.axis_index("height")
    has_prev = tm > 0
    has_next = tm < tm_size - 1
    has_up = ht > 0
    has_down = ht < height_size - 1

    load_lat = pltpu.make_async_copy(lat, latv, load_sem.at[0])
    load_w1 = pltpu.make_async_copy(w1_hbm, w1, load_sem.at[1])
    load_w2 = pltpu.make_async_copy(w2_hbm, w2, load_sem.at[2])
    load_lat.start()
    load_w1.start()
    load_w2.start()

    nxt = jnp.minimum(tm + 1, tm_size - 1)
    prv = jnp.maximum(tm - 1, 0)
    up = jnp.maximum(ht - 1, 0)
    down = jnp.minimum(ht + 1, height_size - 1)

    barrier = pltpu.get_barrier_semaphore()
    for exists, there in (
        (has_prev, {"tm": prv}), (has_next, {"tm": nxt}),
        (has_up, {"height": up}), (has_down, {"height": down}),
    ):
        @pl.when(exists)
        def _(there=there):
            pl.semaphore_signal(barrier, inc=1, device_id=there, device_id_type=MESH)
    peers = sum(h.astype(jnp.int32) for h in (has_prev, has_next, has_up, has_down))
    pl.semaphore_wait(barrier, peers)

    def source(e, row):
        return lat.at[:, row] if e == 0 else sendbuf.at[row]

    def tm_copy(e, row):
        return pltpu.make_async_remote_copy(
            src_ref=source(e, row), dst_ref=halo.at[e, row + 1],
            send_sem=tm_send.at[e, row], recv_sem=tm_recv.at[e, row],
            device_id={"tm": nxt}, device_id_type=MESH)

    def local_edge(e, side):
        return pltpu.make_async_remote_copy(
            src_ref=source(e, 0 if side == 0 else rows - 1), dst_ref=ledge.at[e, side],
            send_sem=hl_send.at[e, side], recv_sem=hl_recv.at[e, side],
            device_id={"height": up if side == 0 else down}, device_id_type=MESH)

    def halo_edge(e, side):
        return pltpu.make_async_remote_copy(
            src_ref=halo.at[e, 1 if side == 0 else rows],
            dst_ref=halo.at[e, rows + 1 if side == 0 else 0],
            send_sem=hf_send.at[e, side], recv_sem=hf_recv.at[e, side],
            device_id={"height": up if side == 0 else down}, device_id_type=MESH)

    to_side = (has_up, has_down)
    from_side = (has_down, has_up)

    def start_tm(e, row):
        @pl.when(has_next)
        def _():
            tm_copy(e, row).start()

    def start_local_edge(e, side):
        @pl.when(to_side[side])
        def _():
            local_edge(e, side).start()

    start_local_edge(0, 0)
    start_local_edge(0, 1)

    def send_row(i, carry):
        start_tm(0, lax.rem(i + rows - 1, rows))
        return carry

    lax.fori_loop(0, rows, send_row, 0)

    g1 = gain1[...].astype(F32).reshape(1, channels)
    g2 = gain2[...].astype(F32).reshape(1, channels)
    b1 = bias1[...].astype(F32).reshape(1, channels)
    b2 = bias2[...].astype(F32).reshape(1, channels)

    def activate(values, gain):
        power = jnp.mean(jnp.square(values), axis=-1, keepdims=True)
        return jax.nn.silu(values * lax.rsqrt(power + EPSILON) * gain)

    pad = jnp.zeros((wide - cells, channels), F32)

    def expand(e, frame, row, values):
        v = jnp.concatenate([values, pad], 0)
        lhs[e, frame, row, :, :channels] = pltpu.roll(v, 1, 0).astype(jnp.bfloat16)
        lhs[e, frame, row, :, channels:2 * channels] = v.astype(jnp.bfloat16)
        lhs[e, frame, row, :, 2 * channels:] = pltpu.roll(v, wide - 1, 0).astype(jnp.bfloat16)

    def clear(e, frame, row):
        lhs[e, frame, row] = jnp.zeros((wide, 3 * channels), jnp.bfloat16)

    def take(e, frame, row, raw):
        values = raw.astype(F32)
        if e == 0:
            values = activate(values, g1)
        expand(e, frame, row, values)

    def take_halo(e, row):
        @pl.when(has_prev)
        def _():
            tm_copy(e, row).wait_recv()
        for side, edge in ((0, 0), (1, rows - 1)):
            if isinstance(row, int) and row == edge:
                @pl.when(has_prev & to_side[side])
                def _(side=side):
                    halo_edge(e, side).start()

        @pl.when(has_prev)
        def _():
            for f in range(2):
                take(e, f, row + 1, halo[e, row + 1, f])

        @pl.when(jnp.logical_not(has_prev))
        def _():
            for f in range(2):
                clear(e, f, row + 1)

    def take_halo_edge(e, side):
        row = rows + 1 if side == 0 else 0
        there = has_prev & from_side[side]

        @pl.when(there)
        def _():
            halo_edge(e, side).wait_recv()
            for f in range(2):
                take(e, f, row, halo[e, row, f])

        @pl.when(jnp.logical_not(there))
        def _():
            for f in range(2):
                clear(e, f, row)

    def take_local_edge(e, side):
        row = rows + 1 if side == 0 else 0

        @pl.when(from_side[side])
        def _():
            local_edge(e, side).wait_recv()
            for f in range(2):
                take(e, 2 + f, row, ledge[e, side, f])

        @pl.when(jnp.logical_not(from_side[side]))
        def _():
            for f in range(2):
                clear(e, 2 + f, row)

    def tap(e, w, frame, row, count, i, j):
        block = lhs[e, frame, pl.ds(row + j, count)].reshape(count * wide, 3 * channels)
        return jnp.dot(block, w[i * 3 + j], preferred_element_type=F32)

    def local_conv(e, w, count):
        def chunk(c, carry):
            row = c * count
            first = sum(tap(e, w, 2, row, count, 2, j) for j in range(3))
            acc[e, 0, pl.ds(row, count)] = first.reshape(count, wide, channels)
            second = sum(
                tap(e, w, 2, row, count, 1, j) + tap(e, w, 3, row, count, 2, j) for j in range(3))
            acc[e, 1, pl.ds(row, count)] = second.reshape(count, wide, channels)
            return carry
        lax.fori_loop(0, rows // count, chunk, 0)

    def halo_conv(e, w, row):
        first = acc[e, 0, row] + sum(
            tap(e, w, 0, row, 1, 0, j) + tap(e, w, 1, row, 1, 1, j) for j in range(3))
        second = acc[e, 1, row] + sum(tap(e, w, 1, row, 1, 0, j) for j in range(3))
        return first[:cells], second[:cells]

    load_lat.wait()

    def own_row(row, carry):
        for f in range(2):
            take(0, 2 + f, row + 1, latv[f, row])
        return carry

    lax.fori_loop(0, rows, own_row, 0)
    take_local_edge(0, 0)
    take_local_edge(0, 1)
    load_w1.wait()
    local_conv(0, w1, 4)

    def middle_row(row):
        for f, v in enumerate(halo_conv(0, w1, row)):
            a = activate((v + b1).astype(jnp.bfloat16).astype(F32), g2)
            sendbuf[row, f] = a.astype(jnp.bfloat16)
            expand(1, 2 + f, row + 1, a)

    take_halo(0, rows - 1)
    take_halo(0, 0)
    take_halo_edge(0, 0)
    take_halo_edge(0, 1)

    def middle_step(r, carry):
        take_halo(0, r)
        middle_row(r - 1)

        @pl.when(r > 1)
        def _():
            start_tm(1, r - 2)
        return carry

    lax.fori_loop(1, rows - 2, middle_step, 0)
    start_local_edge(1, 0)
    take_halo(0, rows - 2)
    start_tm(1, rows - 4)
    middle_row(rows - 1)
    middle_row(rows - 3)
    start_tm(1, rows - 1)
    start_local_edge(1, 1)
    middle_row(rows - 2)
    start_tm(1, rows - 3)
    take_local_edge(1, 0)
    start_tm(1, rows - 2)
    take_local_edge(1, 1)
    load_w2.wait()
    local_conv(1, w2, 4)

    def last_row(row):
        for f, v in enumerate(halo_conv(1, w2, row)):
            out[f, row] = (latv[f, row].astype(F32) + (v + b2)).astype(jnp.bfloat16)

    take_halo(1, 0)

    def last_step(r, carry):
        take_halo(1, r)

        @pl.when(r > 1)
        def _():
            last_row(r - 1)
        return carry

    lax.fori_loop(1, rows - 3, last_step, 0)
    take_halo(1, rows - 1)
    take_halo(1, rows - 3)
    last_row(rows - 4)
    take_halo_edge(1, 1)
    last_row(0)
    take_halo_edge(1, 0)
    take_halo(1, rows - 2)
    last_row(rows - 3)
    last_row(rows - 2)
    last_row(rows - 1)

    def drain(row, carry):
        @pl.when(has_next)
        def _():
            tm_copy(0, row).wait_send()
            tm_copy(1, row).wait_send()
        return carry

    lax.fori_loop(0, rows, drain, 0)
    for e in range(2):
        for side in range(2):
            @pl.when(to_side[side])
            def _(e=e, side=side):
                local_edge(e, side).wait_send()

            @pl.when(has_prev & to_side[side])
            def _(e=e, side=side):
                halo_edge(e, side).wait_send()


def per_device(
    tm_size, height_size,
    latents, first_gain, first_kernel, first_bias, second_gain, second_kernel, second_bias,
):
    frames, rows, cells, channels = latents.shape
    wide = -(-(cells + 1) // 16) * 16
    vmem = pl.BlockSpec(memory_space=pltpu.VMEM)
    hbm = pl.BlockSpec(memory_space=pltpu.HBM)
    bf16 = jnp.bfloat16
    dma = pltpu.SemaphoreType.DMA
    taps = lambda k: k.reshape(9, 3 * channels, channels)
    return pl.pallas_call(
        functools.partial(kernel, tm_size, height_size),
        out_shape=jax.ShapeDtypeStruct(latents.shape, bf16),
        in_specs=[hbm, vmem, vmem, vmem, vmem, hbm, hbm],
        out_specs=vmem,
        scratch_shapes=[
            pltpu.VMEM(latents.shape, bf16),
            pltpu.VMEM((9, 3 * channels, channels), bf16),
            pltpu.VMEM((9, 3 * channels, channels), bf16),
            pltpu.VMEM((2, rows + 2, 2, cells, channels), bf16),
            pltpu.VMEM((2, 2, 2, cells, channels), bf16),
            pltpu.VMEM((rows, 2, cells, channels), bf16),
            pltpu.VMEM((2, 4, rows + 2, wide, 3 * channels), bf16),
            pltpu.VMEM((2, 2, rows, wide, channels), F32),
            dma((3,)),
            dma((2, rows)), dma((2, rows)),
            dma((2, 2)), dma((2, 2)), dma((2, 2)), dma((2, 2)),
        ],
        compiler_params=pltpu.CompilerParams(
            collective_id=0, has_side_effects=True, vmem_limit_bytes=60 * 1024 * 1024),
        name="residual_block",
    )(latents, first_gain, second_gain, first_bias, second_bias,
      taps(first_kernel), taps(second_kernel))


def solution(mesh):
    return jax.shard_map(
        functools.partial(per_device, mesh.shape["tm"], mesh.shape["height"]),
        mesh=mesh,
        in_specs=(P("tm", "height", None, None), P(), P(), P(), P(), P(), P()),
        out_specs=P("tm", "height", None, None),
        check_vma=False,
    )
```

```python
import functools

import jax
import jax.numpy as jnp
from jax import lax
from jax.experimental import pallas as pl
from jax.experimental.pallas import tpu as pltpu
from jax.sharding import PartitionSpec as P

EPSILON = 1e-06
MESH = pl.DeviceIdType.MESH
F32 = jnp.float32
RING = 4
DETOURS = 2


def kernel(
    tm_size, height_size,
    lat, gain1, gain2, bias1, bias2, w1_hbm, w2_hbm,
    out,
    latv, w1, w2, halo, ledge, sendbuf, lhs, acc, relay,
    load_sem, tm_send, tm_recv, hl_send, hl_recv, hf_send, hf_recv, relay_send, relay_recv,
):
    frames, rows, cells, channels = latv.shape
    wide = lhs.shape[3]
    tm = lax.axis_index("tm")
    ht = lax.axis_index("height")
    has_prev = tm > 0
    has_next = tm < tm_size - 1
    has_up = ht > 0
    has_down = ht < height_size - 1

    load_lat = pltpu.make_async_copy(lat, latv, load_sem.at[0])
    load_w1 = pltpu.make_async_copy(w1_hbm, w1, load_sem.at[1])
    load_w2 = pltpu.make_async_copy(w2_hbm, w2, load_sem.at[2])
    load_lat.start()
    load_w1.start()
    load_w2.start()

    nxt = jnp.minimum(tm + 1, tm_size - 1)
    prv = jnp.maximum(tm - 1, 0)
    x = lax.rem(tm, RING)
    base = tm - x
    left = base + lax.rem(x + RING - 1, RING)
    right = base + lax.rem(x + 1, RING)
    right2 = base + lax.rem(x + 2, RING)
    crosses = (x == RING - 1) & has_next
    crossed = (x == 0) & has_prev
    relays_over = (x == 1) & (tm + 3 < tm_size)
    up = jnp.maximum(ht - 1, 0)
    down = jnp.minimum(ht + 1, height_size - 1)

    barrier = pltpu.get_barrier_semaphore()
    for exists, there in (
        (None, {"tm": left}), (None, {"tm": right}),
        (crosses, {"tm": nxt}), (crossed, {"tm": prv}),
        (relays_over, {"tm": jnp.minimum(tm + 3, tm_size - 1)}),
        (crossed, {"tm": jnp.maximum(tm - 3, 0)}),
        (has_up, {"height": up}), (has_down, {"height": down}),
    ):
        if exists is None:
            pl.semaphore_signal(barrier, inc=1, device_id=there, device_id_type=MESH)
            continue

        @pl.when(exists)
        def _(there=there):
            pl.semaphore_signal(barrier, inc=1, device_id=there, device_id_type=MESH)
    peers = 2 + sum(
        h.astype(jnp.int32)
        for h in (crosses, crossed, relays_over, crossed, has_up, has_down))
    pl.semaphore_wait(barrier, peers)

    def source(e, row):
        return lat.at[:, row] if e == 0 else sendbuf.at[row]

    def tm_copy(e, row):
        return pltpu.make_async_remote_copy(
            src_ref=source(e, row), dst_ref=halo.at[e, row + 1],
            send_sem=tm_send.at[e, row], recv_sem=tm_recv.at[e, row],
            device_id={"tm": nxt}, device_id_type=MESH)

    def detour_row(e, k):
        return (rows - 3 if e == 0 else 0) + k

    def hop_copy(hop, e, k):
        row = detour_row(e, k)
        last = hop == 2
        return pltpu.make_async_remote_copy(
            src_ref=source(e, row) if hop == 0 else relay.at[hop - 1, e, k],
            dst_ref=halo.at[e, row + 1] if last else relay.at[hop, e, k],
            send_sem=relay_send.at[hop, e, k],
            recv_sem=tm_recv.at[e, row] if last else relay_recv.at[hop, e, k],
            device_id={"tm": jnp.minimum(right2 + 1, tm_size - 1) if last else left},
            device_id_type=MESH)

    hop_runs = (has_next, right < tm_size - 1, right2 < tm_size - 1)

    def start_detour(e, k):
        @pl.when(hop_runs[0])
        def _():
            hop_copy(0, e, k).start()

    def pass_on(hop, e, k):
        @pl.when(hop_runs[hop])
        def _():
            hop_copy(hop - 1, e, k).wait_recv()
            hop_copy(hop, e, k).start()

    def local_edge(e, side):
        return pltpu.make_async_remote_copy(
            src_ref=source(e, 0 if side == 0 else rows - 1), dst_ref=ledge.at[e, side],
            send_sem=hl_send.at[e, side], recv_sem=hl_recv.at[e, side],
            device_id={"height": up if side == 0 else down}, device_id_type=MESH)

    def halo_edge(e, side):
        return pltpu.make_async_remote_copy(
            src_ref=halo.at[e, 1 if side == 0 else rows],
            dst_ref=halo.at[e, rows + 1 if side == 0 else 0],
            send_sem=hf_send.at[e, side], recv_sem=hf_recv.at[e, side],
            device_id={"height": up if side == 0 else down}, device_id_type=MESH)

    to_side = (has_up, has_down)
    from_side = (has_down, has_up)

    def start_tm(e, row):
        @pl.when(has_next)
        def _():
            tm_copy(e, row).start()

    def start_local_edge(e, side):
        @pl.when(to_side[side])
        def _():
            local_edge(e, side).start()

    for k in range(DETOURS):
        start_detour(0, k)
    start_local_edge(0, 0)
    start_local_edge(0, 1)

    def send_row(i, carry):
        start_tm(0, lax.rem(i + rows - 1, rows))
        return carry

    lax.fori_loop(0, rows - DETOURS, send_row, 0)

    g1 = gain1[...].astype(F32).reshape(1, channels)
    g2 = gain2[...].astype(F32).reshape(1, channels)
    b1 = bias1[...].astype(F32).reshape(1, channels)
    b2 = bias2[...].astype(F32).reshape(1, channels)

    def activate(values, gain):
        power = jnp.mean(jnp.square(values), axis=-1, keepdims=True)
        return jax.nn.silu(values * lax.rsqrt(power + EPSILON) * gain)

    pad = jnp.zeros((wide - cells, channels), F32)

    def expand(e, frame, row, values):
        v = jnp.concatenate([values, pad], 0)
        lhs[e, frame, row, :, :channels] = pltpu.roll(v, 1, 0).astype(jnp.bfloat16)
        lhs[e, frame, row, :, channels:2 * channels] = v.astype(jnp.bfloat16)
        lhs[e, frame, row, :, 2 * channels:] = pltpu.roll(v, wide - 1, 0).astype(jnp.bfloat16)

    def clear(e, frame, row):
        lhs[e, frame, row] = jnp.zeros((wide, 3 * channels), jnp.bfloat16)

    def take(e, frame, row, raw):
        values = raw.astype(F32)
        if e == 0:
            values = activate(values, g1)
        expand(e, frame, row, values)

    def take_halo(e, row):
        @pl.when(has_prev)
        def _():
            tm_copy(e, row).wait_recv()
        for side, edge in ((0, 0), (1, rows - 1)):
            if isinstance(row, int) and row == edge:
                @pl.when(has_prev & to_side[side])
                def _(side=side):
                    halo_edge(e, side).start()

        @pl.when(has_prev)
        def _():
            for f in range(2):
                take(e, f, row + 1, halo[e, row + 1, f])

        @pl.when(jnp.logical_not(has_prev))
        def _():
            for f in range(2):
                clear(e, f, row + 1)

    def take_halo_edge(e, side):
        row = rows + 1 if side == 0 else 0
        there = has_prev & from_side[side]

        @pl.when(there)
        def _():
            halo_edge(e, side).wait_recv()
            for f in range(2):
                take(e, f, row, halo[e, row, f])

        @pl.when(jnp.logical_not(there))
        def _():
            for f in range(2):
                clear(e, f, row)

    def take_local_edge(e, side):
        row = rows + 1 if side == 0 else 0

        @pl.when(from_side[side])
        def _():
            local_edge(e, side).wait_recv()
            for f in range(2):
                take(e, 2 + f, row, ledge[e, side, f])

        @pl.when(jnp.logical_not(from_side[side]))
        def _():
            for f in range(2):
                clear(e, 2 + f, row)

    def tap(e, w, frame, row, count, i, j):
        block = lhs[e, frame, pl.ds(row + j, count)].reshape(count * wide, 3 * channels)
        return jnp.dot(block, w[i * 3 + j], preferred_element_type=F32)

    def local_conv(e, w, count):
        def chunk(c, carry):
            row = c * count
            pass_on(1 + e, e, c)
            first = sum(tap(e, w, 2, row, count, 2, j) for j in range(3))
            acc[e, 0, pl.ds(row, count)] = first.reshape(count, wide, channels)
            second = sum(
                tap(e, w, 2, row, count, 1, j) + tap(e, w, 3, row, count, 2, j) for j in range(3))
            acc[e, 1, pl.ds(row, count)] = second.reshape(count, wide, channels)
            return carry
        lax.fori_loop(0, rows // count, chunk, 0)

    def halo_conv(e, w, row):
        first = acc[e, 0, row] + sum(
            tap(e, w, 0, row, 1, 0, j) + tap(e, w, 1, row, 1, 1, j) for j in range(3))
        second = acc[e, 1, row] + sum(tap(e, w, 1, row, 1, 0, j) for j in range(3))
        return first[:cells], second[:cells]

    load_lat.wait()

    def own_row(row, carry):
        for f in range(2):
            take(0, 2 + f, row + 1, latv[f, row])
        return carry

    lax.fori_loop(0, rows, own_row, 0)
    take_local_edge(0, 0)
    take_local_edge(0, 1)
    load_w1.wait()
    local_conv(0, w1, 4)

    def middle_row(row):
        for f, v in enumerate(halo_conv(0, w1, row)):
            a = activate((v + b1).astype(jnp.bfloat16).astype(F32), g2)
            sendbuf[row, f] = a.astype(jnp.bfloat16)
            expand(1, 2 + f, row + 1, a)

    take_halo(0, rows - 1)
    take_halo(0, 0)
    take_halo_edge(0, 0)
    take_halo_edge(0, 1)
    pass_on(2, 0, 0)

    def middle_step(r, carry):
        take_halo(0, r)
        middle_row(r - 1)

        @pl.when(r == 1)
        def _():
            pass_on(2, 0, 1)

        @pl.when(r == 2)
        def _():
            start_detour(1, 0)
            start_local_edge(1, 0)

        @pl.when(r == 3)
        def _():
            start_detour(1, 1)

        @pl.when(r > 3)
        def _():
            start_tm(1, r - 2)
        return carry

    lax.fori_loop(1, rows - 3, middle_step, 0)
    take_halo(0, rows - 3)
    start_tm(1, rows - 5)
    pass_on(1, 1, 0)
    take_halo(0, rows - 2)

    def late_row(i):
        return rows - 4 + lax.rem(i + 3, 4)

    def late_step(i, carry):
        middle_row(late_row(i))

        @pl.when(i == 0)
        def _():
            pass_on(1, 1, 1)

        @pl.when(i == 1)
        def _():
            start_local_edge(1, 1)

        @pl.when(i > 0)
        def _():
            start_tm(1, late_row(i - 1 + 4))
        return carry

    lax.fori_loop(0, 4, late_step, 0)
    take_local_edge(1, 0)
    start_tm(1, rows - 2)
    take_local_edge(1, 1)
    load_w2.wait()
    local_conv(1, w2, 4)

    def last_row(row):
        for f, v in enumerate(halo_conv(1, w2, row)):
            out[f, row] = (latv[f, row].astype(F32) + (v + b2)).astype(jnp.bfloat16)

    def last_rows(first, count, step):
        def body(i, carry):
            last_row(first + step * i)
            return carry
        lax.fori_loop(0, count, body, 0)

    take_halo(1, 2)
    take_halo(1, 3)
    take_halo(1, rows - 1)
    take_halo(1, 0)
    take_halo(1, 4)
    last_row(3)
    take_halo(1, 1)
    last_rows(2, 2, -1)
    take_halo(1, 5)
    last_row(4)
    take_halo_edge(1, 1)
    last_row(0)
    take_halo_edge(1, 0)
    take_halo(1, 6)
    last_rows(5, 3, 1)

    def drain(i, carry):
        @pl.when(has_next)
        def _():
            tm_copy(0, lax.rem(i + rows - 1, rows)).wait_send()
            tm_copy(1, i + DETOURS).wait_send()
        return carry

    lax.fori_loop(0, rows - DETOURS, drain, 0)
    for hop in range(3):
        @pl.when(hop_runs[hop])
        def _(hop=hop):
            for e in range(2):
                for k in range(DETOURS):
                    hop_copy(hop, e, k).wait_send()

    for e in range(2):
        for side in range(2):
            @pl.when(to_side[side])
            def _(e=e, side=side):
                local_edge(e, side).wait_send()

            @pl.when(has_prev & to_side[side])
            def _(e=e, side=side):
                halo_edge(e, side).wait_send()


def per_device(
    tm_size, height_size,
    latents, first_gain, first_kernel, first_bias, second_gain, second_kernel, second_bias,
):
    frames, rows, cells, channels = latents.shape
    wide = -(-(cells + 1) // 16) * 16
    vmem = pl.BlockSpec(memory_space=pltpu.VMEM)
    hbm = pl.BlockSpec(memory_space=pltpu.HBM)
    bf16 = jnp.bfloat16
    dma = pltpu.SemaphoreType.DMA
    taps = lambda k: k.reshape(9, 3 * channels, channels)
    return pl.pallas_call(
        functools.partial(kernel, tm_size, height_size),
        out_shape=jax.ShapeDtypeStruct(latents.shape, bf16),
        in_specs=[hbm, vmem, vmem, vmem, vmem, hbm, hbm],
        out_specs=vmem,
        scratch_shapes=[
            pltpu.VMEM(latents.shape, bf16),
            pltpu.VMEM((9, 3 * channels, channels), bf16),
            pltpu.VMEM((9, 3 * channels, channels), bf16),
            pltpu.VMEM((2, rows + 2, 2, cells, channels), bf16),
            pltpu.VMEM((2, 2, 2, cells, channels), bf16),
            pltpu.VMEM((rows, 2, cells, channels), bf16),
            pltpu.VMEM((2, 4, rows + 2, wide, 3 * channels), bf16),
            pltpu.VMEM((2, 2, rows, wide, channels), F32),
            pltpu.VMEM((2, 2, DETOURS, 2, cells, channels), bf16),
            dma((3,)),
            dma((2, rows)), dma((2, rows)),
            dma((2, 2)), dma((2, 2)), dma((2, 2)), dma((2, 2)),
            dma((3, 2, DETOURS)), dma((2, 2, DETOURS)),
        ],
        compiler_params=pltpu.CompilerParams(
            collective_id=0, has_side_effects=True, vmem_limit_bytes=60 * 1024 * 1024),
        name="residual_block",
    )(latents, first_gain, second_gain, first_bias, second_bias,
      taps(first_kernel), taps(second_kernel))


def solution(mesh):
    return jax.shard_map(
        functools.partial(per_device, mesh.shape["tm"], mesh.shape["height"]),
        mesh=mesh,
        in_specs=(P("tm", "height", None, None), P(), P(), P(), P(), P(), P()),
        out_specs=P("tm", "height", None, None),
        check_vma=False,
    )
```

```python
import functools

import jax
import jax.numpy as jnp
from jax import lax
from jax.experimental import pallas as pl
from jax.experimental.pallas import tpu as pltpu
from jax.sharding import PartitionSpec as P

EPSILON = 1e-06
MESH = pl.DeviceIdType.MESH
F32 = jnp.float32
RING = 4
DETOURS = 2


def kernel(
    tm_size, height_size,
    lat, gain1, gain2, bias1, bias2, w1_hbm, w2_hbm,
    out,
    latv, w1, w2, halo, ledge, sendbuf, lhs, acc, relay,
    load_sem, tm_send, tm_recv, hl_send, hl_recv, hf_send, hf_recv, relay_send, relay_recv,
):
    frames, rows, cells, channels = latv.shape
    wide = lhs.shape[3]
    tm = lax.axis_index("tm")
    ht = lax.axis_index("height")
    has_prev = tm > 0
    has_next = tm < tm_size - 1
    has_up = ht > 0
    has_down = ht < height_size - 1

    load_lat = pltpu.make_async_copy(lat, latv, load_sem.at[0])
    load_w1 = pltpu.make_async_copy(w1_hbm, w1, load_sem.at[1])
    load_w2 = pltpu.make_async_copy(w2_hbm, w2, load_sem.at[2])
    load_lat.start()
    load_w1.start()
    load_w2.start()

    nxt = jnp.minimum(tm + 1, tm_size - 1)
    prv = jnp.maximum(tm - 1, 0)
    x = lax.rem(tm, RING)
    base = tm - x
    left = base + lax.rem(x + RING - 1, RING)
    right = base + lax.rem(x + 1, RING)
    right2 = base + lax.rem(x + 2, RING)
    crosses = (x == RING - 1) & has_next
    crossed = (x == 0) & has_prev
    relays_over = (x == 1) & (tm + 3 < tm_size)
    up = jnp.maximum(ht - 1, 0)
    down = jnp.minimum(ht + 1, height_size - 1)

    barrier = pltpu.get_barrier_semaphore()
    for exists, there in (
        (None, {"tm": left}), (None, {"tm": right}),
        (crosses, {"tm": nxt}), (crossed, {"tm": prv}),
        (relays_over, {"tm": jnp.minimum(tm + 3, tm_size - 1)}),
        (crossed, {"tm": jnp.maximum(tm - 3, 0)}),
        (has_up, {"height": up}), (has_down, {"height": down}),
    ):
        if exists is None:
            pl.semaphore_signal(barrier, inc=1, device_id=there, device_id_type=MESH)
            continue

        @pl.when(exists)
        def _(there=there):
            pl.semaphore_signal(barrier, inc=1, device_id=there, device_id_type=MESH)
    peers = 2 + sum(
        h.astype(jnp.int32)
        for h in (crosses, crossed, relays_over, crossed, has_up, has_down))
    pl.semaphore_wait(barrier, peers)

    def source(e, row):
        return lat.at[:, row] if e == 0 else sendbuf.at[row]

    def tm_copy(e, row):
        return pltpu.make_async_remote_copy(
            src_ref=source(e, row), dst_ref=halo.at[e, row + 1],
            send_sem=tm_send.at[e, row], recv_sem=tm_recv.at[e, row],
            device_id={"tm": nxt}, device_id_type=MESH)

    def detour_row(e, k):
        return (rows - 3 if e == 0 else 0) + k

    def hop_copy(hop, e, k):
        row = detour_row(e, k)
        last = hop == 2
        return pltpu.make_async_remote_copy(
            src_ref=source(e, row) if hop == 0 else relay.at[hop - 1, e, k],
            dst_ref=halo.at[e, row + 1] if last else relay.at[hop, e, k],
            send_sem=relay_send.at[hop, e, k],
            recv_sem=tm_recv.at[e, row] if last else relay_recv.at[hop, e, k],
            device_id={"tm": jnp.minimum(right2 + 1, tm_size - 1) if last else left},
            device_id_type=MESH)

    hop_runs = (has_next, right < tm_size - 1, right2 < tm_size - 1)

    def start_detour(e, k):
        @pl.when(hop_runs[0])
        def _():
            hop_copy(0, e, k).start()

    def pass_on(hop, e, k):
        @pl.when(hop_runs[hop])
        def _():
            hop_copy(hop - 1, e, k).wait_recv()
            hop_copy(hop, e, k).start()

    def local_edge(e, side):
        return pltpu.make_async_remote_copy(
            src_ref=source(e, 0 if side == 0 else rows - 1), dst_ref=ledge.at[e, side],
            send_sem=hl_send.at[e, side], recv_sem=hl_recv.at[e, side],
            device_id={"height": up if side == 0 else down}, device_id_type=MESH)

    def halo_edge(e, side):
        return pltpu.make_async_remote_copy(
            src_ref=halo.at[e, 1 if side == 0 else rows],
            dst_ref=halo.at[e, rows + 1 if side == 0 else 0],
            send_sem=hf_send.at[e, side], recv_sem=hf_recv.at[e, side],
            device_id={"height": up if side == 0 else down}, device_id_type=MESH)

    to_side = (has_up, has_down)
    from_side = (has_down, has_up)

    def start_tm(e, row):
        @pl.when(has_next)
        def _():
            tm_copy(e, row).start()

    def start_local_edge(e, side):
        @pl.when(to_side[side])
        def _():
            local_edge(e, side).start()

    for k in range(DETOURS):
        start_detour(0, k)
    start_local_edge(0, 0)
    start_local_edge(0, 1)

    def send_row(i, carry):
        start_tm(0, lax.rem(i + rows - 1, rows))
        return carry

    lax.fori_loop(0, rows - DETOURS, send_row, 0)

    g1 = gain1[...].astype(F32).reshape(1, channels)
    g2 = gain2[...].astype(F32).reshape(1, channels)
    b1 = bias1[...].astype(F32).reshape(1, channels)
    b2 = bias2[...].astype(F32).reshape(1, channels)

    def activate(values, gain):
        power = jnp.mean(jnp.square(values), axis=-1, keepdims=True)
        return jax.nn.silu(values * lax.rsqrt(power + EPSILON) * gain)

    pad = jnp.zeros((wide - cells, channels), F32)

    def expand(e, frame, row, values):
        v = jnp.concatenate([values, pad], 0)
        lhs[e, frame, row, :, :channels] = pltpu.roll(v, 1, 0).astype(jnp.bfloat16)
        lhs[e, frame, row, :, channels:2 * channels] = v.astype(jnp.bfloat16)
        lhs[e, frame, row, :, 2 * channels:] = pltpu.roll(v, wide - 1, 0).astype(jnp.bfloat16)

    def clear(e, frame, row):
        lhs[e, frame, row] = jnp.zeros((wide, 3 * channels), jnp.bfloat16)

    def take(e, frame, row, raw):
        values = raw.astype(F32)
        if e == 0:
            values = activate(values, g1)
        expand(e, frame, row, values)

    def take_halo(e, row):
        @pl.when(has_prev)
        def _():
            tm_copy(e, row).wait_recv()
        for side, edge in ((0, 0), (1, rows - 1)):
            if isinstance(row, int) and row == edge:
                @pl.when(has_prev & to_side[side])
                def _(side=side):
                    halo_edge(e, side).start()

        @pl.when(has_prev)
        def _():
            for f in range(2):
                take(e, f, row + 1, halo[e, row + 1, f])

        @pl.when(jnp.logical_not(has_prev))
        def _():
            for f in range(2):
                clear(e, f, row + 1)

    def take_halo_edge(e, side):
        row = rows + 1 if side == 0 else 0
        there = has_prev & from_side[side]

        @pl.when(there)
        def _():
            halo_edge(e, side).wait_recv()
            for f in range(2):
                take(e, f, row, halo[e, row, f])

        @pl.when(jnp.logical_not(there))
        def _():
            for f in range(2):
                clear(e, f, row)

    def take_local_edge(e, side):
        row = rows + 1 if side == 0 else 0

        @pl.when(from_side[side])
        def _():
            local_edge(e, side).wait_recv()
            for f in range(2):
                take(e, 2 + f, row, ledge[e, side, f])

        @pl.when(jnp.logical_not(from_side[side]))
        def _():
            for f in range(2):
                clear(e, 2 + f, row)

    def tap(e, w, frame, row, count, i, j):
        block = lhs[e, frame, pl.ds(row + j, count)].reshape(count * wide, 3 * channels)
        return jnp.dot(block, w[i * 3 + j], preferred_element_type=F32)

    def local_conv(e, w, count):
        def chunk(c, carry):
            row = c * count
            pass_on(1 + e, e, c)
            first = sum(tap(e, w, 2, row, count, 2, j) for j in range(3))
            acc[e, 0, pl.ds(row, count)] = first.reshape(count, wide, channels)
            second = sum(
                tap(e, w, 2, row, count, 1, j) + tap(e, w, 3, row, count, 2, j) for j in range(3))
            acc[e, 1, pl.ds(row, count)] = second.reshape(count, wide, channels)
            return carry
        lax.fori_loop(0, rows // count, chunk, 0)

    def halo_conv(e, w, row, count):
        shape = (count, wide, channels)

        def both(j):
            block = lhs[e, 0:2, pl.ds(row + j, count)].reshape(2 * count * wide, 3 * channels)
            return jnp.dot(block, w[j], preferred_element_type=F32)

        pair = sum(both(j) for j in range(3)).reshape(2, *shape)
        middle = sum(tap(e, w, 1, row, count, 1, j) for j in range(3)).reshape(shape)
        first = acc[e, 0, pl.ds(row, count)] + pair[0] + middle
        second = acc[e, 1, pl.ds(row, count)] + pair[1]
        return first[:, :cells], second[:, :cells]

    load_lat.wait()

    def own_row(row, carry):
        for f in range(2):
            take(0, 2 + f, row + 1, latv[f, row])
        return carry

    lax.fori_loop(0, rows, own_row, 0)
    take_local_edge(0, 0)
    take_local_edge(0, 1)
    load_w1.wait()
    local_conv(0, w1, 4)

    def middle_rows(row, count):
        for f, v in enumerate(halo_conv(0, w1, row, count)):
            for c in range(count):
                a = activate((v[c] + b1).astype(jnp.bfloat16).astype(F32), g2)
                sendbuf[row + c, f] = a.astype(jnp.bfloat16)
                expand(1, 2 + f, row + c + 1, a)

    take_halo(0, rows - 1)
    take_halo(0, 0)
    take_halo_edge(0, 0)
    take_halo_edge(0, 1)
    pass_on(2, 0, 0)

    def middle_step(r, carry):
        take_halo(0, r)
        middle_rows(r - 1, 1)

        @pl.when(r == 1)
        def _():
            pass_on(2, 0, 1)

        @pl.when(r == 2)
        def _():
            start_detour(1, 0)
            start_local_edge(1, 0)

        @pl.when(r == 3)
        def _():
            start_detour(1, 1)

        @pl.when(r > 3)
        def _():
            start_tm(1, r - 2)
        return carry

    lax.fori_loop(1, rows - 3, middle_step, 0)
    take_halo(0, rows - 3)
    start_tm(1, rows - 5)
    pass_on(1, 1, 0)
    take_halo(0, rows - 2)

    middle_rows(rows - 2, 2)
    pass_on(1, 1, 1)
    take_local_edge(1, 0)
    start_tm(1, rows - 1)
    start_local_edge(1, 1)
    start_tm(1, rows - 2)
    middle_rows(rows - 4, 2)
    take_local_edge(1, 1)
    start_tm(1, rows - 3)
    start_tm(1, rows - 4)
    load_w2.wait()
    local_conv(1, w2, 4)

    def last_rows(row, count):
        for f, v in enumerate(halo_conv(1, w2, row, count)):
            for c in range(count):
                out[f, row + c] = (
                    latv[f, row + c].astype(F32) + (v[c] + b2)).astype(jnp.bfloat16)

    take_halo(1, 2)
    take_halo(1, 3)
    take_halo(1, rows - 1)
    take_halo(1, 0)
    take_halo(1, 1)
    last_rows(1, 2)
    take_halo_edge(1, 1)
    last_rows(0, 1)
    take_halo(1, 6)
    take_halo_edge(1, 0)
    take_halo(1, 5)
    last_rows(6, 2)
    take_halo(1, 4)
    last_rows(3, 3)

    def drain(i, carry):
        @pl.when(has_next)
        def _():
            tm_copy(0, lax.rem(i + rows - 1, rows)).wait_send()
            tm_copy(1, i + DETOURS).wait_send()
        return carry

    lax.fori_loop(0, rows - DETOURS, drain, 0)
    for hop in range(3):
        @pl.when(hop_runs[hop])
        def _(hop=hop):
            for e in range(2):
                for k in range(DETOURS):
                    hop_copy(hop, e, k).wait_send()

    for e in range(2):
        for side in range(2):
            @pl.when(to_side[side])
            def _(e=e, side=side):
                local_edge(e, side).wait_send()

            @pl.when(has_prev & to_side[side])
            def _(e=e, side=side):
                halo_edge(e, side).wait_send()


def per_device(
    tm_size, height_size,
    latents, first_gain, first_kernel, first_bias, second_gain, second_kernel, second_bias,
):
    frames, rows, cells, channels = latents.shape
    wide = -(-(cells + 1) // 16) * 16
    vmem = pl.BlockSpec(memory_space=pltpu.VMEM)
    hbm = pl.BlockSpec(memory_space=pltpu.HBM)
    bf16 = jnp.bfloat16
    dma = pltpu.SemaphoreType.DMA
    taps = lambda k: k.reshape(9, 3 * channels, channels)
    return pl.pallas_call(
        functools.partial(kernel, tm_size, height_size),
        out_shape=jax.ShapeDtypeStruct(latents.shape, bf16),
        in_specs=[hbm, vmem, vmem, vmem, vmem, hbm, hbm],
        out_specs=vmem,
        scratch_shapes=[
            pltpu.VMEM(latents.shape, bf16),
            pltpu.VMEM((9, 3 * channels, channels), bf16),
            pltpu.VMEM((9, 3 * channels, channels), bf16),
            pltpu.VMEM((2, rows + 2, 2, cells, channels), bf16),
            pltpu.VMEM((2, 2, 2, cells, channels), bf16),
            pltpu.VMEM((rows, 2, cells, channels), bf16),
            pltpu.VMEM((2, 4, rows + 2, wide, 3 * channels), bf16),
            pltpu.VMEM((2, 2, rows, wide, channels), F32),
            pltpu.VMEM((2, 2, DETOURS, 2, cells, channels), bf16),
            dma((3,)),
            dma((2, rows)), dma((2, rows)),
            dma((2, 2)), dma((2, 2)), dma((2, 2)), dma((2, 2)),
            dma((3, 2, DETOURS)), dma((2, 2, DETOURS)),
        ],
        compiler_params=pltpu.CompilerParams(
            collective_id=0, has_side_effects=True, vmem_limit_bytes=60 * 1024 * 1024),
        name="residual_block",
    )(latents, first_gain, second_gain, first_bias, second_bias,
      taps(first_kernel), taps(second_kernel))


def solution(mesh):
    return jax.shard_map(
        functools.partial(per_device, mesh.shape["tm"], mesh.shape["height"]),
        mesh=mesh,
        in_specs=(P("tm", "height", None, None), P(), P(), P(), P(), P(), P()),
        out_specs=P("tm", "height", None, None),
        check_vma=False,
    )
```

```python
import functools

import jax
import jax.numpy as jnp
from jax import lax
from jax.experimental import pallas as pl
from jax.experimental.pallas import tpu as pltpu
from jax.sharding import PartitionSpec as P

EPSILON = 1e-06
MESH = pl.DeviceIdType.MESH
F32 = jnp.float32
RING = 4
DETOURS = (2, 1)


def kernel(
    tm_size, height_size,
    lat, gain1, gain2, bias1, bias2, w1_hbm, w2_hbm,
    out,
    latv, w1, w2, halo, ledge, sendbuf, lhs, acc, relay,
    load_sem, tm_send, tm_recv, hl_send, hl_recv, hf_send, hf_recv, relay_send, relay_recv,
):
    frames, rows, cells, channels = latv.shape
    wide = lhs.shape[3]
    tm = lax.axis_index("tm")
    ht = lax.axis_index("height")
    has_prev = tm > 0
    has_next = tm < tm_size - 1
    has_up = ht > 0
    has_down = ht < height_size - 1

    load_lat = pltpu.make_async_copy(lat, latv, load_sem.at[0])
    load_w1 = pltpu.make_async_copy(w1_hbm, w1, load_sem.at[1])
    load_w2 = pltpu.make_async_copy(w2_hbm, w2, load_sem.at[2])
    load_lat.start()
    load_w1.start()
    load_w2.start()

    nxt = jnp.minimum(tm + 1, tm_size - 1)
    prv = jnp.maximum(tm - 1, 0)
    x = lax.rem(tm, RING)
    base = tm - x
    left = base + lax.rem(x + RING - 1, RING)
    right = base + lax.rem(x + 1, RING)
    right2 = base + lax.rem(x + 2, RING)
    crosses = (x == RING - 1) & has_next
    crossed = (x == 0) & has_prev
    relays_over = (x == 1) & (tm + 3 < tm_size)
    up = jnp.maximum(ht - 1, 0)
    down = jnp.minimum(ht + 1, height_size - 1)

    barrier = pltpu.get_barrier_semaphore()
    for exists, there in (
        (None, {"tm": left}), (None, {"tm": right}),
        (crosses, {"tm": nxt}), (crossed, {"tm": prv}),
        (relays_over, {"tm": jnp.minimum(tm + 3, tm_size - 1)}),
        (crossed, {"tm": jnp.maximum(tm - 3, 0)}),
        (has_up, {"height": up}), (has_down, {"height": down}),
    ):
        if exists is None:
            pl.semaphore_signal(barrier, inc=1, device_id=there, device_id_type=MESH)
            continue

        @pl.when(exists)
        def _(there=there):
            pl.semaphore_signal(barrier, inc=1, device_id=there, device_id_type=MESH)
    peers = 2 + sum(
        h.astype(jnp.int32)
        for h in (crosses, crossed, relays_over, crossed, has_up, has_down))
    pl.semaphore_wait(barrier, peers)

    def source(e, row):
        return lat.at[:, row] if e == 0 else sendbuf.at[row]

    def tm_copy(e, row):
        return pltpu.make_async_remote_copy(
            src_ref=source(e, row), dst_ref=halo.at[e, row + 1],
            send_sem=tm_send.at[e, row], recv_sem=tm_recv.at[e, row],
            device_id={"tm": nxt}, device_id_type=MESH)

    def detour_row(e, k):
        return (rows - 3 if e == 0 else 0) + k

    def hop_copy(hop, e, k):
        row = detour_row(e, k)
        last = hop == 2
        return pltpu.make_async_remote_copy(
            src_ref=source(e, row) if hop == 0 else relay.at[hop - 1, e, k],
            dst_ref=halo.at[e, row + 1] if last else relay.at[hop, e, k],
            send_sem=relay_send.at[hop, e, k],
            recv_sem=tm_recv.at[e, row] if last else relay_recv.at[hop, e, k],
            device_id={"tm": jnp.minimum(right2 + 1, tm_size - 1) if last else left},
            device_id_type=MESH)

    hop_runs = (has_next, right < tm_size - 1, right2 < tm_size - 1)

    def start_detour(e, k):
        @pl.when(hop_runs[0])
        def _():
            hop_copy(0, e, k).start()

    def pass_on(hop, e, k):
        @pl.when(hop_runs[hop])
        def _():
            hop_copy(hop - 1, e, k).wait_recv()
            hop_copy(hop, e, k).start()

    def local_edge(e, side):
        return pltpu.make_async_remote_copy(
            src_ref=source(e, 0 if side == 0 else rows - 1), dst_ref=ledge.at[e, side],
            send_sem=hl_send.at[e, side], recv_sem=hl_recv.at[e, side],
            device_id={"height": up if side == 0 else down}, device_id_type=MESH)

    def halo_edge(e, side):
        return pltpu.make_async_remote_copy(
            src_ref=halo.at[e, 1 if side == 0 else rows],
            dst_ref=halo.at[e, rows + 1 if side == 0 else 0],
            send_sem=hf_send.at[e, side], recv_sem=hf_recv.at[e, side],
            device_id={"height": up if side == 0 else down}, device_id_type=MESH)

    to_side = (has_up, has_down)
    from_side = (has_down, has_up)

    def start_tm(e, row):
        @pl.when(has_next)
        def _():
            tm_copy(e, row).start()

    def start_local_edge(e, side):
        @pl.when(to_side[side])
        def _():
            local_edge(e, side).start()

    for k in range(DETOURS[0]):
        start_detour(0, k)
    start_local_edge(0, 0)
    start_local_edge(0, 1)

    def send_row(i, carry):
        start_tm(0, lax.rem(i + rows - 1, rows))
        return carry

    lax.fori_loop(0, rows - DETOURS[0], send_row, 0)

    g1 = gain1[...].astype(F32).reshape(1, channels)
    g2 = gain2[...].astype(F32).reshape(1, channels)
    b1 = bias1[...].astype(F32).reshape(1, channels)
    b2 = bias2[...].astype(F32).reshape(1, channels)

    def activate(values, gain):
        power = jnp.mean(jnp.square(values), axis=-1, keepdims=True)
        return jax.nn.silu(values * lax.rsqrt(power + EPSILON) * gain)

    pad = jnp.zeros((wide - cells, channels), F32)

    def expand(e, frame, row, values):
        v = jnp.concatenate([values, pad], 0)
        lhs[e, frame, row, :, :channels] = pltpu.roll(v, 1, 0).astype(jnp.bfloat16)
        lhs[e, frame, row, :, channels:2 * channels] = v.astype(jnp.bfloat16)
        lhs[e, frame, row, :, 2 * channels:] = pltpu.roll(v, wide - 1, 0).astype(jnp.bfloat16)

    def clear(e, frame, row):
        lhs[e, frame, row] = jnp.zeros((wide, 3 * channels), jnp.bfloat16)

    def take(e, frame, row, raw):
        values = raw.astype(F32)
        if e == 0:
            values = activate(values, g1)
        expand(e, frame, row, values)

    def take_halo(e, row):
        @pl.when(has_prev)
        def _():
            tm_copy(e, row).wait_recv()
        for side, edge in ((0, 0), (1, rows - 1)):
            if isinstance(row, int) and row == edge:
                @pl.when(has_prev & to_side[side])
                def _(side=side):
                    halo_edge(e, side).start()

        @pl.when(has_prev)
        def _():
            for f in range(2):
                take(e, f, row + 1, halo[e, row + 1, f])

        @pl.when(jnp.logical_not(has_prev))
        def _():
            for f in range(2):
                clear(e, f, row + 1)

    def take_halo_edge(e, side):
        row = rows + 1 if side == 0 else 0
        there = has_prev & from_side[side]

        @pl.when(there)
        def _():
            halo_edge(e, side).wait_recv()
            for f in range(2):
                take(e, f, row, halo[e, row, f])

        @pl.when(jnp.logical_not(there))
        def _():
            for f in range(2):
                clear(e, f, row)

    def take_local_edge(e, side):
        row = rows + 1 if side == 0 else 0

        @pl.when(from_side[side])
        def _():
            local_edge(e, side).wait_recv()
            for f in range(2):
                take(e, 2 + f, row, ledge[e, side, f])

        @pl.when(jnp.logical_not(from_side[side]))
        def _():
            for f in range(2):
                clear(e, 2 + f, row)

    def tap(e, w, frame, row, count, i, j):
        block = lhs[e, frame, pl.ds(row + j, count)].reshape(count * wide, 3 * channels)
        return jnp.dot(block, w[i * 3 + j], preferred_element_type=F32)

    def local_conv(e, w, count):
        def chunk(c, carry):
            row = c * count
            if e == 0:
                pass_on(1, 0, c)
            first = sum(tap(e, w, 2, row, count, 2, j) for j in range(3))
            acc[e, 0, pl.ds(row, count)] = first.reshape(count, wide, channels)
            second = sum(
                tap(e, w, 2, row, count, 1, j) + tap(e, w, 3, row, count, 2, j) for j in range(3))
            acc[e, 1, pl.ds(row, count)] = second.reshape(count, wide, channels)
            return carry
        lax.fori_loop(0, rows // count, chunk, 0)

    def halo_conv(e, w, row):
        first = acc[e, 0, row] + sum(
            tap(e, w, 0, row, 1, 0, j) + tap(e, w, 1, row, 1, 1, j) for j in range(3))
        second = acc[e, 1, row] + sum(tap(e, w, 1, row, 1, 0, j) for j in range(3))
        return first[:cells], second[:cells]

    load_lat.wait()

    def own_row(row, carry):
        for f in range(2):
            take(0, 2 + f, row + 1, latv[f, row])
        return carry

    lax.fori_loop(0, rows, own_row, 0)
    take_local_edge(0, 0)
    take_local_edge(0, 1)
    load_w1.wait()
    local_conv(0, w1, 4)

    def middle_row(row):
        for f, v in enumerate(halo_conv(0, w1, row)):
            a = activate((v + b1).astype(jnp.bfloat16).astype(F32), g2)
            sendbuf[row, f] = a.astype(jnp.bfloat16)
            expand(1, 2 + f, row + 1, a)

    take_halo(0, rows - 1)
    take_halo(0, 0)
    take_halo_edge(0, 0)
    take_halo_edge(0, 1)
    pass_on(2, 0, 0)

    def middle_step(r, carry):
        take_halo(0, r)
        middle_row(r - 1)

        @pl.when(r == 1)
        def _():
            pass_on(2, 0, 1)

        @pl.when(r == 2)
        def _():
            start_detour(1, 0)
            start_local_edge(1, 0)

        @pl.when(r == 3)
        def _():
            start_tm(1, 1)

        @pl.when(r > 3)
        def _():
            start_tm(1, r - 2)
        return carry

    lax.fori_loop(1, rows - 3, middle_step, 0)
    take_halo(0, rows - 3)
    start_tm(1, rows - 5)
    pass_on(1, 1, 0)
    take_halo(0, rows - 2)

    def late_row(i):
        return rows - 4 + lax.rem(i + 3, 4)

    def late_step(i, carry):
        middle_row(late_row(i))

        @pl.when(i == 1)
        def _():
            start_local_edge(1, 1)

        @pl.when(i > 0)
        def _():
            start_tm(1, late_row(i - 1 + 4))
        return carry

    lax.fori_loop(0, 4, late_step, 0)
    take_local_edge(1, 0)
    start_tm(1, rows - 2)
    take_local_edge(1, 1)
    load_w2.wait()
    pass_on(2, 1, 0)
    local_conv(1, w2, 4)

    def last_row(row):
        for f, v in enumerate(halo_conv(1, w2, row)):
            out[f, row] = (latv[f, row].astype(F32) + (v + b2)).astype(jnp.bfloat16)

    def last_rows(first, count, step):
        def body(i, carry):
            last_row(first + step * i)
            return carry
        lax.fori_loop(0, count, body, 0)

    take_halo(1, 1)
    take_halo(1, 2)
    take_halo(1, 3)
    last_row(2)
    take_halo(1, rows - 1)
    take_halo(1, 4)
    last_row(3)
    take_halo(1, 0)
    take_halo(1, 5)
    last_rows(4, 2, -3)
    take_halo_edge(1, 1)
    last_row(0)
    take_halo_edge(1, 0)
    take_halo(1, 6)
    last_rows(5, 3, 1)

    def drain(i, carry):
        @pl.when(has_next)
        def _():
            tm_copy(0, lax.rem(i + rows - 1, rows)).wait_send()
            tm_copy(1, i + 1).wait_send()
        return carry

    lax.fori_loop(0, rows - DETOURS[0], drain, 0)

    @pl.when(has_next)
    def _():
        tm_copy(1, rows - 1).wait_send()

    for hop in range(3):
        @pl.when(hop_runs[hop])
        def _(hop=hop):
            for e in range(2):
                for k in range(DETOURS[e]):
                    hop_copy(hop, e, k).wait_send()

    for e in range(2):
        for side in range(2):
            @pl.when(to_side[side])
            def _(e=e, side=side):
                local_edge(e, side).wait_send()

            @pl.when(has_prev & to_side[side])
            def _(e=e, side=side):
                halo_edge(e, side).wait_send()


def per_device(
    tm_size, height_size,
    latents, first_gain, first_kernel, first_bias, second_gain, second_kernel, second_bias,
):
    frames, rows, cells, channels = latents.shape
    wide = -(-(cells + 1) // 16) * 16
    vmem = pl.BlockSpec(memory_space=pltpu.VMEM)
    hbm = pl.BlockSpec(memory_space=pltpu.HBM)
    bf16 = jnp.bfloat16
    dma = pltpu.SemaphoreType.DMA
    taps = lambda k: k.reshape(9, 3 * channels, channels)
    return pl.pallas_call(
        functools.partial(kernel, tm_size, height_size),
        out_shape=jax.ShapeDtypeStruct(latents.shape, bf16),
        in_specs=[hbm, vmem, vmem, vmem, vmem, hbm, hbm],
        out_specs=vmem,
        scratch_shapes=[
            pltpu.VMEM(latents.shape, bf16),
            pltpu.VMEM((9, 3 * channels, channels), bf16),
            pltpu.VMEM((9, 3 * channels, channels), bf16),
            pltpu.VMEM((2, rows + 2, 2, cells, channels), bf16),
            pltpu.VMEM((2, 2, 2, cells, channels), bf16),
            pltpu.VMEM((rows, 2, cells, channels), bf16),
            pltpu.VMEM((2, 4, rows + 2, wide, 3 * channels), bf16),
            pltpu.VMEM((2, 2, rows, wide, channels), F32),
            pltpu.VMEM((2, 2, DETOURS[0], 2, cells, channels), bf16),
            dma((3,)),
            dma((2, rows)), dma((2, rows)),
            dma((2, 2)), dma((2, 2)), dma((2, 2)), dma((2, 2)),
            dma((3, 2, DETOURS[0])), dma((2, 2, DETOURS[0])),
        ],
        compiler_params=pltpu.CompilerParams(
            collective_id=0, has_side_effects=True, vmem_limit_bytes=60 * 1024 * 1024),
        name="residual_block",
    )(latents, first_gain, second_gain, first_bias, second_bias,
      taps(first_kernel), taps(second_kernel))


def solution(mesh):
    return jax.shard_map(
        functools.partial(per_device, mesh.shape["tm"], mesh.shape["height"]),
        mesh=mesh,
        in_specs=(P("tm", "height", None, None), P(), P(), P(), P(), P(), P()),
        out_specs=P("tm", "height", None, None),
        check_vma=False,
    )
```
